256 devices in a mesh: task: 16 (over z_lo, y, core), rows: 16 (over z_hi, x).
Axes of the slice: x: 4, y: 4, z: 8 (z_hi: 4, z_lo: 2; z = z_hi * 2 + z_lo), core: 2. Of those that a mesh axis runs over, the one named last changes fastest.
Arguments:
- probes: bfloat16 [16, 384, 8192], P('task', None, 'rows'), may hold values from -48 to 48
- task_weights: bfloat16 [16, 8192, 128], P('task', 'rows'), may hold values from -6 to 6
Outputs:
- merged: float32 [8192, 128], P(('rows', 'task'))
- residual: float32 [8192, 128], P(('rows', 'task'))
The draws below stay inside these ranges and needn't reach their ends.
All inputs are finite; a program needn't handle non-finite values.
Results may differ from the reference program's by a relative error of at most 0.0003.
Values may be sent and summed in bfloat16 or wider, within the bound.
No kernel may reach another device: no remote copies, remote signals or barrier semaphores. Data moves between devices by JAX's collectives and lax.ppermute only.
A program may use at most 128 MiB of HBM per device.

```python
import math
import jax
import jax.numpy as jnp
from jax import lax

D = 8192
PROBE = 384
COLS = 128
ITERS = 2
TASKS = 16


def draw_probes(key, part):
    k_base, k_col, k_row = jax.random.split(key, 3)
    ramp = jnp.arange(D, dtype=jnp.float32) / max(D - 1, 1)
    colscale = (1.0 + 2.0 * ramp) * jnp.exp(jax.random.uniform(k_col, (D,), jnp.float32, 0.0, math.log(3.0))) / 3.0
    rowscale = jnp.exp(jax.random.uniform(k_row, (TASKS, PROBE, 1), jnp.float32, 0.0, math.log(4.0))) / 2.0
    base = jnp.clip(jax.random.normal(k_base, (TASKS, PROBE, D), jnp.float32), -5.0, 5.0)
    return (base * rowscale * colscale[None, None, :]).astype(jnp.bfloat16)


def steps_of(own_key, dims, cuts, least, top_value):
    level = 1.0
    for dim, parts in cuts:
        draws = jax.random.uniform(jax.random.fold_in(jax.random.fold_in(own_key, 6), dim), (parts,), jnp.float32, least / len(cuts), top_value / len(cuts))
        level = level * jnp.repeat(jnp.exp(draws), dims[dim] // parts).reshape((-1,) + (1,) * (len(dims) - 1 - dim))
    return level


def bell_draw(stream_key, dims, scale, bound, cuts=(), kind=jnp.bfloat16):
    result = jax.random.normal(stream_key, dims, jnp.float32) * scale
    if len(cuts) > 0:
        result = steps_of(stream_key, dims, cuts, -0.22, 0.18) * result
    return jnp.clip(result, min=-bound, max=bound).astype(kind)


def setup_inputs(seed: int = 0) -> dict:
    streams_of = jax.random.split(jax.random.key(seed), 3)
    probes = draw_probes(jax.random.fold_in(streams_of[2], 71), 0)
    task_weights = bell_draw(streams_of[1], (TASKS, D, COLS), 1.0, 6.0, ((0, 16), (1, 16)))
    return dict(probes=probes, task_weights=task_weights)


ALPHA = 0.9
EPS = 1e-6


def reference(probes, task_weights):
    scale = 1.0 / (PROBE * TASKS)

    def accumulate(carry, item):
        acc_sys, acc_tgt, acc_diag = carry
        x, w = item
        g = jnp.dot(x.T, x, preferred_element_type=jnp.float32)
        d = jnp.diagonal(g)
        y = jnp.dot(x, w, preferred_element_type=jnp.float32)
        b = ALPHA * jnp.einsum("pd,pc->dc", x.astype(jnp.float32), y, precision=lax.Precision.HIGHEST)
        b = b + (1.0 - ALPHA) * d[:, None] * w.astype(jnp.float32)
        return (acc_sys + (ALPHA * scale) * g, acc_tgt + scale * b, acc_diag + ((1.0 - ALPHA) * scale) * d), None

    init = (jnp.zeros((D, D), jnp.float32), jnp.zeros((D, COLS), jnp.float32), jnp.zeros((D,), jnp.float32))
    (system, targets, diag_sum), _ = lax.scan(accumulate, init, (probes, task_weights))
    idx = jnp.arange(D, dtype=jnp.int32)
    system = system.at[idx, idx].add(diag_sum)

    merged = jnp.zeros((D, COLS), jnp.float32)
    residual = targets
    direction = targets
    norm_now = jnp.sum(residual * residual, axis=0)
    for step in range(ITERS):
        image = jnp.dot(system, direction, precision=lax.Precision.HIGHEST)
        alpha = norm_now / jnp.sum(direction * image, axis=0)
        merged = merged + alpha * direction
        residual = residual - alpha * image
        norm_next = jnp.sum(residual * residual, axis=0)
        direction = residual + (norm_next / (norm_now + EPS)) * direction
        norm_now = norm_next
    return merged, residual
```

```python
import jax
import jax.numpy as jnp
from jax import lax
from jax.sharding import PartitionSpec as P

ALPHA = 0.9
EPS = 1e-06


def scatter_sum(chunks, axis):
    return jnp.sum(lax.all_to_all(chunks, axis, 0, 0), axis=0)


def gather(chunk, axis):
    n = lax.axis_size(axis)
    copies = jnp.broadcast_to(chunk[None], (n,) + chunk.shape)
    return lax.all_to_all(copies, axis, 0, 0).reshape(n * chunk.shape[0], chunk.shape[1])


def pieces(value):
    high = lax.reduce_precision(value, 8, 7)
    low = value - high
    return jnp.concatenate([high.astype(jnp.bfloat16), low.astype(jnp.bfloat16)], axis=1)


def times(x, value, dim):
    cols = value.shape[1]
    wide = lax.dot_general(x, pieces(value), (((dim,), (0,)), ((), ())), preferred_element_type=jnp.float32)
    return wide[:, :cols] + wide[:, cols:]


def with_rows(value, axis, rows):
    n = lax.axis_size(axis)
    chunks = value.reshape(n, value.shape[0] // n, value.shape[1])
    extra = jnp.concatenate([r[None] for r in rows] + [jnp.zeros((8 - len(rows), value.shape[1]), jnp.float32)])
    return jnp.concatenate([chunks, jnp.broadcast_to(extra[None], (n,) + extra.shape)], axis=1)


def on_device(probes, task_weights):
    x = probes[0]
    w = task_weights[0]
    tokens, width = x.shape
    tasks = lax.axis_size("task")
    scale = 1.0 / (tokens * tasks)
    gram_scale, diag_scale = ALPHA * scale, (1.0 - ALPHA) * scale
    wide_x = x.astype(jnp.float32)
    diag = diag_scale * jnp.sum(wide_x * wide_x, axis=0)[:, None]

    def columns(value):
        return jnp.sum(value, axis=0)

    first = jnp.dot(x, w, preferred_element_type=jnp.float32)
    first = scatter_sum(first.reshape(-1, tokens // lax.axis_size("rows"), first.shape[1]), "rows")
    outputs = gather(first, "rows")
    part = gram_scale * times(x, outputs, 0) + diag * w.astype(jnp.float32)
    target_chunk = scatter_sum(part.reshape(tasks, width // tasks, part.shape[1]), "task")
    target = gather(target_chunk, "task")

    share = tokens // lax.axis_size("rows")
    rows = with_rows(times(x, target, 1), "rows", [columns(target * target), columns(diag * target * target)])
    rows = scatter_sum(rows, "rows")
    norm0, weigh0 = rows[share], rows[share + 1]
    image0 = gather(rows[:share], "rows")
    part = gram_scale * times(x, image0, 0) + diag * target
    curve = gram_scale * columns(image0 * image0) + weigh0
    part = scatter_sum(with_rows(part, "task", [curve]), "task")
    depth = width // tasks
    alpha0 = norm0 / part[depth]
    residual_chunk = target_chunk - alpha0 * part[:depth]
    residual = gather(residual_chunk, "task")

    rows = with_rows(
        times(x, residual, 1),
        "rows",
        [columns(residual * residual), columns(diag * residual * residual), columns(diag * residual * target)],
    )
    rows = scatter_sum(rows, "rows")
    norm1, weigh1, cross = rows[share], rows[share + 1], rows[share + 2]
    beta = norm1 / (norm0 + EPS)
    image1 = gather(rows[:share], "rows") + beta * image0
    direction = residual + beta * target
    part = gram_scale * times(x, image1, 0) + diag * direction
    curve = gram_scale * columns(image1 * image1) + weigh1 + 2.0 * beta * cross + beta * beta * weigh0
    part = scatter_sum(with_rows(part, "task", [curve]), "task")
    alpha1 = norm1 / part[depth]
    merged = alpha0 * target_chunk + alpha1 * (residual_chunk + beta * target_chunk)
    return merged, residual_chunk - alpha1 * part[:depth]


def solution(mesh):
    in_specs = (P("task", None, "rows"), P("task", "rows", None))
    out_specs = (P(("rows", "task"), None), P(("rows", "task"), None))
    return jax.shard_map(
        on_device, mesh=mesh, in_specs=in_specs, out_specs=out_specs, check_vma=False
    )
```

```python
import jax
import jax.numpy as jnp
from jax import lax
from jax.sharding import PartitionSpec as P


ALPHA = 0.9
EPS = 1e-06


def moved(value, axis, to):
    return lax.ppermute(value, axis, [(i, to(i)) for i in range(16)])


def x_move(value, k):
    return moved(value, "rows", lambda r: r - r % 4 + (r + k) % 4)


def zhi_sum(value):
    return value + sum(moved(value, "rows", lambda r, k=k: (r + 4 * k) % 16) for k in (1, 3, 2))


def core_move(value):
    return moved(value, "task", lambda t: t ^ 1)


def zlo_move(value):
    return moved(value, "task", lambda t: t ^ 8)


def y_move(value, k):
    return moved(value, "task", lambda t: (t & 9) | ((((t >> 1) & 3) + k) % 4) << 1)


def pick(value, index, dim=0):
    return lax.dynamic_index_in_dim(value, index, dim, keepdims=False)


def pieces(value):
    high = lax.reduce_precision(value, 8, 7)
    low = value - high
    return jnp.concatenate([high.astype(jnp.bfloat16), low.astype(jnp.bfloat16)], axis=0)


def product(value, x, dim):
    n = value.shape[0]
    wide = lax.dot_general(pieces(value), x, (((1,), (dim,)), ((), ())), preferred_element_type=jnp.float32)
    return wide[:n] + wide[n:]


def blocks_of(value):
    return value.reshape(value.shape[0], -1, 128).transpose(1, 0, 2)


def flat(blocks):
    return blocks.transpose(1, 0, 2).reshape(blocks.shape[1], -1)


def halves(blocks, core):
    grid = blocks.reshape((2, 2, 4) + blocks.shape[1:])
    own, other = pick(grid, core, 1), pick(grid, 1 - core, 1)
    return own.reshape((8,) + blocks.shape[1:]), other.reshape((8,) + blocks.shape[1:])


def whole(own, core):
    other = core_move(own)
    shape = own.shape[1:]
    own, other = own.reshape((2, 1, 4) + shape), other.reshape((2, 1, 4) + shape)
    pair = jnp.where(core == 0, jnp.concatenate([own, other], 1), jnp.concatenate([other, own], 1))
    return pair.reshape((16,) + shape)


def task_half_sum(blocks, extra, core):
    own, other = halves(blocks, core)
    if extra is not None:
        own, other = jnp.concatenate([own, extra[None]]), jnp.concatenate([other, extra[None]])
    own = own + core_move(other)
    own = own + zlo_move(own)
    return own + y_move(own, 1) + y_move(own, 3) + y_move(own, 2)


def with_scalars(value, scalars):
    lane = lax.broadcasted_iota(jnp.int32, (value.shape[0], 128), 1)
    extra = jnp.zeros((value.shape[0], 128), jnp.float32)
    for i, s in enumerate(scalars):
        extra = jnp.where(lane == i, s, extra)
    return jnp.concatenate([value, extra], axis=1)


def total(value):
    return jnp.sum(value, axis=1, keepdims=True)


def on_device(probes, task_weights):
    own_x = probes[0]
    w = task_weights[0]
    tokens, width = own_x.shape
    tasks = lax.axis_size("task")
    row = lax.axis_index("rows")
    task = lax.axis_index("task")
    x, core, ylow, yhigh, zlo = row % 4, task % 2, (task // 2) % 2, (task // 4) % 2, task // 8
    scale = 1.0 / (tokens * tasks)
    gram_scale, diag_scale = ALPHA * scale, (1.0 - ALPHA) * scale

    half = tokens // 2
    from_left = x_move(own_x, 1)
    from_right = x_move(own_x, 3)

    first = lax.dot_general(w, own_x, (((0,), (1,)), ((), ())), preferred_element_type=jnp.float32)
    first = first.reshape(4, 32, tokens)
    mine = pick(first, x)
    for k in (1, 3, 2):
        mine = mine + x_move(pick(first, (x + k) % 4), k)
    turned = w.T.reshape(4, 32, width)
    weights = [pick(turned, x)]
    for k in (1, 2, 3):
        weights.append(x_move(pick(turned, (x + k) % 4), k))
    outputs = mine
    for k in (1, 3, 2):
        outputs = outputs + moved(mine, "rows", lambda r, k=k: (r + 4 * k) % 16)
    far_left = x_move(from_left[:half], 1)
    far_right = x_move(from_right[half:], 3)

    xs = jnp.concatenate([own_x, from_left, jnp.concatenate([far_left, far_right]), from_right], axis=1)
    ws = jnp.concatenate(weights, axis=1)
    wide_x = xs.astype(jnp.float32)
    diag = diag_scale * jnp.sum(wide_x * wide_x, axis=0, keepdims=True)

    def image_part(y, vector):
        return blocks_of(gram_scale * product(y, xs, 0) + diag * vector)

    part = task_half_sum(image_part(outputs, ws.astype(jnp.float32)), None, core)
    target_blocks = whole(part, core)
    target = flat(target_blocks)

    scalars = [total(target * target), total(diag * target * target)]
    rows = zhi_sum(with_scalars(product(target, xs, 1), scalars))
    image0, norm0, weigh0 = rows[:, :tokens], rows[:, tokens : tokens + 1], rows[:, tokens + 1 : tokens + 2]
    curve = jnp.broadcast_to(gram_scale * total(image0 * image0) + weigh0, (32, 128))
    part = task_half_sum(image_part(image0, target), curve, core)
    alpha0 = norm0 / part[8][:, :1]
    residual_half = halves(target_blocks, core)[0] - alpha0[None] * part[:8]
    residual_blocks = whole(residual_half, core)
    residual = flat(residual_blocks)

    scalars = [total(residual * residual), total(diag * residual * residual), total(diag * residual * target)]
    rows = zhi_sum(with_scalars(product(residual, xs, 1), scalars))
    norm1, weigh1, cross = (rows[:, tokens + i : tokens + i + 1] for i in range(3))
    beta = norm1 / (norm0 + EPS)
    image1 = rows[:, :tokens] + beta * image0
    direction = residual + beta * target
    curve = gram_scale * total(image1 * image1) + weigh1 + 2.0 * beta * cross + beta * beta * weigh0
    curve = jnp.broadcast_to(curve, (1, 32, 128))

    part = image_part(image1, direction)
    own = jnp.concatenate([part, curve])
    own = (own + core_move(own)).reshape(17, 32, 128)
    grid, curve = own[:16].reshape(4, 2, 2, 32, 128), own[16:]
    own, other = pick(grid, zlo, 1).reshape(8, 32, 128), pick(grid, 1 - zlo, 1).reshape(8, 32, 128)
    own = jnp.concatenate([own, curve]) + zlo_move(jnp.concatenate([other, curve]))
    grid, curve = own[:8].reshape(4, 2, 32, 128), own[8:]
    y = 2 * yhigh + ylow

    def for_y(k):
        return jnp.concatenate([pick(grid, ((y + k) % 4) // 2, 1), curve])

    own = for_y(0) + y_move(for_y(1), 1) + y_move(for_y(3), 3) + y_move(for_y(2), 2)
    alpha1 = norm1 / own[4][:, :1]

    def mine_of(blocks):
        return pick(blocks.reshape(4, 4, 32, 128), 2 * zlo + yhigh, 1)

    my_target, my_residual = mine_of(target_blocks), mine_of(residual_blocks)
    merged = alpha0 * my_target + alpha1 * (my_residual + beta * my_target)
    both = jnp.concatenate([merged, my_residual - alpha1 * own[:4]], axis=1)
    both = lax.dynamic_slice_in_dim(both, 32 * (2 * ylow + core), 32, 2)

    groups = jnp.stack([both[0]] + [x_move(both[k], 4 - k) for k in (1, 2, 3)])
    groups = lax.dynamic_slice_in_dim(jnp.concatenate([groups, groups]), (4 - x) % 4, 4, 0)
    return groups[:, :32].reshape(128, 32).T, groups[:, 32:].reshape(128, 32).T


def solution(mesh):
    in_specs = (P("task", None, "rows"), P("task", "rows", None))
    out_specs = (P(("rows", "task"), None), P(("rows", "task"), None))

    return jax.shard_map(on_device, mesh=mesh, in_specs=in_specs, out_specs=out_specs, check_vma=False)
```

```python
import jax
import jax.numpy as jnp
from jax import lax
from jax.sharding import PartitionSpec as P


ALPHA = 0.9
EPS = 1e-06


def moved(value, axis, to):
    return lax.ppermute(value, axis, [(i, to(i)) for i in range(16)])


def x_move(value, k):
    return moved(value, "rows", lambda r: r - r % 4 + (r + k) % 4)


def zhi_sum(value):
    return value + sum(moved(value, "rows", lambda r, k=k: (r + 4 * k) % 16) for k in (1, 3, 2))


def core_move(value):
    return moved(value, "task", lambda t: t ^ 1)


def zlo_move(value):
    return moved(value, "task", lambda t: t ^ 8)


def y_move(value, k):
    return moved(value, "task", lambda t: (t & 9) | ((((t >> 1) & 3) + k) % 4) << 1)


def pick(value, index, dim=0):
    return lax.dynamic_index_in_dim(value, index, dim, keepdims=False)


def pieces(value):
    high = lax.reduce_precision(value, 8, 7)
    low = value - high
    return jnp.concatenate([high.astype(jnp.bfloat16), low.astype(jnp.bfloat16)], axis=0)


def product(value, x, dim):
    n = value.shape[0]
    wide = lax.dot_general(pieces(value), x, (((1,), (dim,)), ((), ())), preferred_element_type=jnp.float32)
    return wide[:n] + wide[n:]


def blocks_of(value):
    return value.reshape(value.shape[0], -1, 128).transpose(1, 0, 2)


def flat(blocks):
    return blocks.transpose(1, 0, 2).reshape(blocks.shape[1], -1)


def halves(blocks, core):
    grid = blocks.reshape((2, 2, 4) + blocks.shape[1:])
    own, other = pick(grid, core, 1), pick(grid, 1 - core, 1)
    return own.reshape((8,) + blocks.shape[1:]), other.reshape((8,) + blocks.shape[1:])


def whole(own, core):
    other = core_move(own)
    shape = own.shape[1:]
    own, other = own.reshape((2, 1, 4) + shape), other.reshape((2, 1, 4) + shape)
    pair = jnp.where(core == 0, jnp.concatenate([own, other], 1), jnp.concatenate([other, own], 1))
    return pair.reshape((16,) + shape)


def task_half_sum(blocks, extra, core):
    own, other = halves(blocks, core)
    if extra is not None:
        own, other = jnp.concatenate([own, extra[None]]), jnp.concatenate([other, extra[None]])
    own = own + core_move(other)
    own = own + zlo_move(own)
    return own + y_move(own, 1) + y_move(own, 3) + y_move(own, 2)


def with_scalars(value, scalars):
    lane = lax.broadcasted_iota(jnp.int32, (value.shape[0], 128), 1)
    extra = jnp.zeros((value.shape[0], 128), jnp.float32)
    for i, s in enumerate(scalars):
        extra = jnp.where(lane == i, s, extra)
    return jnp.concatenate([value, extra], axis=1)


def total(value):
    return jnp.sum(value, axis=1, keepdims=True)


def on_device(probes, task_weights):
    own_x = probes[0]
    w = task_weights[0]
    tokens, width = own_x.shape
    tasks = lax.axis_size("task")
    row = lax.axis_index("rows")
    task = lax.axis_index("task")
    x, core, ylow, yhigh, zlo = row % 4, task % 2, (task // 2) % 2, (task // 4) % 2, task // 8
    scale = 1.0 / (tokens * tasks)
    gram_scale, diag_scale = ALPHA * scale, (1.0 - ALPHA) * scale

    half = tokens // 2
    from_left = x_move(own_x, 1)
    from_right = x_move(own_x, 3)

    first = lax.dot_general(w, own_x, (((0,), (1,)), ((), ())), preferred_element_type=jnp.float32)
    first = first.reshape(4, 32, tokens)
    mine = pick(first, x)
    for k in (1, 3, 2):
        mine = mine + x_move(pick(first, (x + k) % 4), k)
    turned = w.T.reshape(4, 32, width)
    ws_far = x_move(pick(turned, (x + 2) % 4), 2)
    far_left = x_move(jnp.concatenate([from_left[:half], pick(turned, (x + 1) % 4)]), 1)
    far_right = x_move(jnp.concatenate([from_right[half:], pick(turned, (x + 3) % 4)]), 3)
    outputs = mine
    for k in (1, 3, 2):
        outputs = outputs + moved(mine, "rows", lambda r, k=k: (r + 4 * k) % 16)

    far = jnp.concatenate([far_left[:half], far_right[:half]])
    xs = jnp.concatenate([own_x, from_left, far, from_right], axis=1)
    ws = jnp.concatenate([pick(turned, x), far_left[half:], ws_far, far_right[half:]], axis=1)
    wide_x = xs.astype(jnp.float32)
    diag = diag_scale * jnp.sum(wide_x * wide_x, axis=0, keepdims=True)

    def image_part(y, vector):
        return blocks_of(gram_scale * product(y, xs, 0) + diag * vector)

    part = task_half_sum(image_part(outputs, ws.astype(jnp.float32)), None, core)
    target_blocks = whole(part, core)
    target = flat(target_blocks)

    scalars = [total(target * target), total(diag * target * target)]
    rows = zhi_sum(with_scalars(product(target, xs, 1), scalars))
    image0, norm0, weigh0 = rows[:, :tokens], rows[:, tokens : tokens + 1], rows[:, tokens + 1 : tokens + 2]
    curve = jnp.broadcast_to(gram_scale * total(image0 * image0) + weigh0, (32, 128))
    part = task_half_sum(image_part(image0, target), curve, core)
    alpha0 = norm0 / part[8][:, :1]
    residual_half = halves(target_blocks, core)[0] - alpha0[None] * part[:8]
    residual_blocks = whole(residual_half, core)
    residual = flat(residual_blocks)

    scalars = [total(residual * residual), total(diag * residual * residual), total(diag * residual * target)]
    rows = zhi_sum(with_scalars(product(residual, xs, 1), scalars))
    norm1, weigh1, cross = (rows[:, tokens + i : tokens + i + 1] for i in range(3))
    beta = norm1 / (norm0 + EPS)
    image1 = rows[:, :tokens] + beta * image0
    direction = residual + beta * target
    curve = gram_scale * total(image1 * image1) + weigh1 + 2.0 * beta * cross + beta * beta * weigh0
    curve = jnp.broadcast_to(curve, (1, 32, 128))

    part = image_part(image1, direction)
    own = jnp.concatenate([part, curve])
    own = (own + core_move(own)).reshape(17, 32, 128)
    grid, curve = own[:16].reshape(4, 2, 2, 32, 128), own[16:]
    own, other = pick(grid, zlo, 1).reshape(8, 32, 128), pick(grid, 1 - zlo, 1).reshape(8, 32, 128)
    own = jnp.concatenate([own, curve]) + zlo_move(jnp.concatenate([other, curve]))
    grid, curve = own[:8].reshape(4, 2, 32, 128), own[8:]
    y = 2 * yhigh + ylow

    def for_y(k):
        return jnp.concatenate([pick(grid, ((y + k) % 4) // 2, 1), curve])

    own = for_y(0) + y_move(for_y(1), 1) + y_move(for_y(3), 3) + y_move(for_y(2), 2)
    alpha1 = norm1 / own[4][:, :1]

    def mine_of(blocks):
        return pick(blocks.reshape(4, 4, 32, 128), 2 * zlo + yhigh, 1)

    my_target, my_residual = mine_of(target_blocks), mine_of(residual_blocks)
    merged = alpha0 * my_target + alpha1 * (my_residual + beta * my_target)
    both = jnp.concatenate([merged, my_residual - alpha1 * own[:4]], axis=1)
    both = lax.dynamic_slice_in_dim(both, 32 * (2 * ylow + core), 32, 2)

    groups = jnp.stack([both[0]] + [x_move(both[k], 4 - k) for k in (1, 2, 3)])
    groups = lax.dynamic_slice_in_dim(jnp.concatenate([groups, groups]), (4 - x) % 4, 4, 0)
    return groups[:, :32].reshape(128, 32).T, groups[:, 32:].reshape(128, 32).T


def solution(mesh):
    in_specs = (P("task", None, "rows"), P("task", "rows", None))
    out_specs = (P(("rows", "task"), None), P(("rows", "task"), None))

    return jax.shard_map(on_device, mesh=mesh, in_specs=in_specs, out_specs=out_specs, check_vma=False)
```

```python
import jax
import jax.numpy as jnp
from jax import lax
from jax.sharding import PartitionSpec as P


ALPHA = 0.9
EPS = 1e-06


def moved(value, axis, to):
    return lax.ppermute(value, axis, [(i, to(i)) for i in range(16)])


def staged(value_of, move):
    arrived = []
    for k in (2, 3, 1):
        arrived.append(move(value_of(k), k))
    return arrived


def x_move(value, k):
    return moved(value, "rows", lambda r: r - r % 4 + (r + k) % 4)


def zhi_move(value, k):
    return moved(value, "rows", lambda r: (r + 4 * k) % 16)


def core_move(value):
    return moved(value, "task", lambda t: t ^ 1)


def zlo_move(value):
    return moved(value, "task", lambda t: t ^ 8)


def y_move(value, k):
    return moved(value, "task", lambda t: (t & 9) | ((((t >> 1) & 3) + k) % 4) << 1)


def sum_over(value, move):
    two, three, one = staged(lambda k: value, move)
    return value + one + three + two


def pick(value, index, dim=0):
    return lax.dynamic_index_in_dim(value, index, dim, keepdims=False)


def pieces(value):
    high = lax.reduce_precision(value, 8, 7)
    low = value - high
    return jnp.concatenate([high.astype(jnp.bfloat16), low.astype(jnp.bfloat16)], axis=0)


def product(value, x, dim):
    n = value.shape[0]
    wide = lax.dot_general(pieces(value), x, (((1,), (dim,)), ((), ())), preferred_element_type=jnp.float32)
    return wide[:n] + wide[n:]


def blocks_of(value):
    return value.reshape(value.shape[0], -1, 128).transpose(1, 0, 2)


def flat(blocks):
    return blocks.transpose(1, 0, 2).reshape(blocks.shape[1], -1)


def halves(blocks, core):
    grid = blocks.reshape((2, 2, 4) + blocks.shape[1:])
    own, other = pick(grid, core, 1), pick(grid, 1 - core, 1)
    return own.reshape((8,) + blocks.shape[1:]), other.reshape((8,) + blocks.shape[1:])


def whole(own, core):
    other = core_move(own)
    shape = own.shape[1:]
    own, other = own.reshape((2, 1, 4) + shape), other.reshape((2, 1, 4) + shape)
    pair = jnp.where(core == 0, jnp.concatenate([own, other], 1), jnp.concatenate([other, own], 1))
    return pair.reshape((16,) + shape)


def task_half_sum(blocks, extra, core):
    own, other = halves(blocks, core)
    if extra is not None:
        own, other = jnp.concatenate([own, extra[None]]), jnp.concatenate([other, extra[None]])
    own = own + core_move(other)
    own = own + zlo_move(own)
    return sum_over(own, y_move)


def with_scalars(value, scalars):
    lane = lax.broadcasted_iota(jnp.int32, (value.shape[0], 128), 1)
    extra = jnp.zeros((value.shape[0], 128), jnp.float32)
    for i, s in enumerate(scalars):
        extra = jnp.where(lane == i, s, extra)
    return jnp.concatenate([value, extra], axis=1)


def total(value):
    return jnp.sum(value, axis=1, keepdims=True)


def on_device(probes, task_weights):
    own_x = probes[0]
    w = task_weights[0]
    tokens, width = own_x.shape
    tasks = lax.axis_size("task")
    row = lax.axis_index("rows")
    task = lax.axis_index("task")
    x, core, ylow, yhigh, zlo = row % 4, task % 2, (task // 2) % 2, (task // 4) % 2, task // 8
    scale = 1.0 / (tokens * tasks)
    gram_scale, diag_scale = ALPHA * scale, (1.0 - ALPHA) * scale

    first = lax.dot_general(w, own_x, (((0,), (1,)), ((), ())), preferred_element_type=jnp.float32)
    first = first.reshape(4, 32, tokens)
    two, three, one = staged(lambda k: pick(first, (x + k) % 4), x_move)
    mine = pick(first, x) + one + three + two
    turned = w.T.reshape(4, 32, width)
    ws_far = x_move(pick(turned, (x + 2) % 4), 2)

    half = tokens // 2
    from_left = x_move(own_x, 1)
    from_right = x_move(own_x, 3)
    outputs = sum_over(mine, zhi_move)
    far_left = x_move(jnp.concatenate([from_left[:half], pick(turned, (x + 1) % 4)]), 1)
    far_right = x_move(jnp.concatenate([from_right[half:], pick(turned, (x + 3) % 4)]), 3)

    far = jnp.concatenate([far_left[:half], far_right[:half]])
    xs = jnp.concatenate([own_x, from_left, far, from_right], axis=1)
    ws = jnp.concatenate([pick(turned, x), far_left[half:], ws_far, far_right[half:]], axis=1)
    wide_x = xs.astype(jnp.float32)
    diag = diag_scale * jnp.sum(wide_x * wide_x, axis=0, keepdims=True)

    def image_part(y, vector):
        return blocks_of(gram_scale * product(y, xs, 0) + diag * vector)

    part = task_half_sum(image_part(outputs, ws.astype(jnp.float32)), None, core)
    target_blocks = whole(part, core)
    target = flat(target_blocks)

    scalars = [total(target * target), total(diag * target * target)]
    rows = sum_over(with_scalars(product(target, xs, 1), scalars), zhi_move)
    image0, norm0, weigh0 = rows[:, :tokens], rows[:, tokens : tokens + 1], rows[:, tokens + 1 : tokens + 2]
    curve = jnp.broadcast_to(gram_scale * total(image0 * image0) + weigh0, (32, 128))
    part = task_half_sum(image_part(image0, target), curve, core)
    alpha0 = norm0 / part[8][:, :1]
    residual_half = halves(target_blocks, core)[0] - alpha0[None] * part[:8]
    residual_blocks = whole(residual_half, core)
    residual = flat(residual_blocks)

    scalars = [total(residual * residual), total(diag * residual * residual), total(diag * residual * target)]
    rows = sum_over(with_scalars(product(residual, xs, 1), scalars), zhi_move)
    norm1, weigh1, cross = (rows[:, tokens + i : tokens + i + 1] for i in range(3))
    beta = norm1 / (norm0 + EPS)
    image1 = rows[:, :tokens] + beta * image0
    direction = residual + beta * target
    curve = gram_scale * total(image1 * image1) + weigh1 + 2.0 * beta * cross + beta * beta * weigh0
    curve = jnp.broadcast_to(curve, (1, 32, 128))

    part = image_part(image1, direction)
    own = jnp.concatenate([part, curve])
    own = (own + core_move(own)).reshape(17, 32, 128)
    grid, curve = own[:16].reshape(4, 2, 2, 32, 128), own[16:]
    own, other = pick(grid, zlo, 1).reshape(8, 32, 128), pick(grid, 1 - zlo, 1).reshape(8, 32, 128)
    own = jnp.concatenate([own, curve]) + zlo_move(jnp.concatenate([other, curve]))
    grid, curve = own[:8].reshape(4, 2, 32, 128), own[8:]
    y = 2 * yhigh + ylow

    def for_y(k):
        return jnp.concatenate([pick(grid, ((y + k) % 4) // 2, 1), curve])

    two, three, one = staged(for_y, y_move)
    own = for_y(0) + one + three + two
    alpha1 = norm1 / own[4][:, :1]

    def mine_of(blocks):
        return pick(blocks.reshape(4, 4, 32, 128), 2 * zlo + yhigh, 1)

    my_target, my_residual = mine_of(target_blocks), mine_of(residual_blocks)
    merged = alpha0 * my_target + alpha1 * (my_residual + beta * my_target)
    both = jnp.concatenate([merged, my_residual - alpha1 * own[:4]], axis=1)
    both = lax.dynamic_slice_in_dim(both, 32 * (2 * ylow + core), 32, 2)

    two, three, one = staged(lambda k: both[4 - k], x_move)
    groups = jnp.stack([both[0], three, two, one])
    groups = lax.dynamic_slice_in_dim(jnp.concatenate([groups, groups]), (4 - x) % 4, 4, 0)
    return groups[:, :32].reshape(128, 32).T, groups[:, 32:].reshape(128, 32).T


def solution(mesh):
    in_specs = (P("task", None, "rows"), P("task", "rows", None))
    out_specs = (P(("rows", "task"), None), P(("rows", "task"), None))

    return jax.shard_map(on_device, mesh=mesh, in_specs=in_specs, out_specs=out_specs, check_vma=False)
```

```python
import jax
import jax.numpy as jnp
from jax import lax
from jax.sharding import PartitionSpec as P


ALPHA = 0.9
EPS = 1e-06


def moved(value, axis, to):
    return lax.ppermute(value, axis, [(i, to(i)) for i in range(16)])


def staged(value_of, move):
    arrived = []
    for k in (2, 3, 1):
        arrived.append(move(value_of(k), k))
    return arrived


def x_move(value, k):
    return moved(value, "rows", lambda r: r - r % 4 + (r + k) % 4)


def zhi_move(value, k):
    return moved(value, "rows", lambda r: (r + 4 * k) % 16)


def core_move(value):
    return moved(value, "task", lambda t: t ^ 1)


def zlo_move(value):
    return moved(value, "task", lambda t: t ^ 8)


def y_move(value, k):
    return moved(value, "task", lambda t: (t & 9) | ((((t >> 1) & 3) + k) % 4) << 1)


def sum_over(value, move):
    two, three, one = staged(lambda k: value, move)
    return value + one + three + two


def pick(value, index, dim=0):
    return lax.dynamic_index_in_dim(value, index, dim, keepdims=False)


def pieces(value):
    high = lax.reduce_precision(value, 8, 7)
    low = value - high
    return jnp.concatenate([high.astype(jnp.bfloat16), low.astype(jnp.bfloat16)], axis=0)


def product(value, x, dim):
    n = value.shape[0]
    wide = lax.dot_general(pieces(value), x, (((1,), (dim,)), ((), ())), preferred_element_type=jnp.float32)
    return wide[:n] + wide[n:]


def blocks_of(value):
    return value.reshape(value.shape[0], -1, 128).transpose(1, 0, 2)


def flat(blocks):
    return blocks.transpose(1, 0, 2).reshape(blocks.shape[1], -1)


def halves(blocks, core):
    grid = blocks.reshape((2, 2, 4) + blocks.shape[1:])
    own, other = pick(grid, core, 1), pick(grid, 1 - core, 1)
    return own.reshape((8,) + blocks.shape[1:]), other.reshape((8,) + blocks.shape[1:])


def whole(own, core):
    other = core_move(own)
    shape = own.shape[1:]
    own, other = own.reshape((2, 1, 4) + shape), other.reshape((2, 1, 4) + shape)
    pair = jnp.where(core == 0, jnp.concatenate([own, other], 1), jnp.concatenate([other, own], 1))
    return pair.reshape((16,) + shape)


def task_half_sum(blocks, extra, core):
    own, other = halves(blocks, core)
    if extra is not None:
        own, other = jnp.concatenate([own, extra[None]]), jnp.concatenate([other, extra[None]])
    own = own + core_move(other)
    own = own + zlo_move(own)
    return sum_over(own, y_move)


def with_scalars(value, scalars):
    lane = lax.broadcasted_iota(jnp.int32, (value.shape[0], 128), 1)
    extra = jnp.zeros((value.shape[0], 128), jnp.float32)
    for i, s in enumerate(scalars):
        extra = jnp.where(lane == i, s, extra)
    return jnp.concatenate([value, extra], axis=1)


def total(value):
    return jnp.sum(value, axis=1, keepdims=True)


def on_device(probes, task_weights):
    own_x = probes[0]
    w = task_weights[0]
    tokens, width = own_x.shape
    tasks = lax.axis_size("task")
    row = lax.axis_index("rows")
    task = lax.axis_index("task")
    x, core = row % 4, task % 2
    scale = 1.0 / (tokens * tasks)
    gram_scale, diag_scale = ALPHA * scale, (1.0 - ALPHA) * scale

    first = lax.dot_general(w, own_x, (((0,), (1,)), ((), ())), preferred_element_type=jnp.float32)
    first = first.reshape(4, 32, tokens)
    two, three, one = staged(lambda k: pick(first, (x + k) % 4), x_move)
    mine = pick(first, x) + one + three + two
    turned = w.T.reshape(4, 32, width)
    ws_far = x_move(pick(turned, (x + 2) % 4), 2)

    half = tokens // 2
    from_left = x_move(own_x, 1)
    from_right = x_move(own_x, 3)
    outputs = sum_over(mine, zhi_move)
    far_left = x_move(jnp.concatenate([from_left[:half], pick(turned, (x + 1) % 4)]), 1)
    far_right = x_move(jnp.concatenate([from_right[half:], pick(turned, (x + 3) % 4)]), 3)

    far = jnp.concatenate([far_left[:half], far_right[:half]])
    xs = jnp.concatenate([own_x, from_left, far, from_right], axis=1)
    ws = jnp.concatenate([pick(turned, x), far_left[half:], ws_far, far_right[half:]], axis=1)
    wide_x = xs.astype(jnp.float32)
    diag = diag_scale * jnp.sum(wide_x * wide_x, axis=0, keepdims=True)

    def image_part(y, vector):
        return blocks_of(gram_scale * product(y, xs, 0) + diag * vector)

    part = task_half_sum(image_part(outputs, ws.astype(jnp.float32)), None, core)
    target_blocks = whole(part, core)
    target = flat(target_blocks)

    scalars = [total(target * target), total(diag * target * target)]
    rows = sum_over(with_scalars(product(target, xs, 1), scalars), zhi_move)
    image0, norm0, weigh0 = rows[:, :tokens], rows[:, tokens : tokens + 1], rows[:, tokens + 1 : tokens + 2]
    curve = jnp.broadcast_to(gram_scale * total(image0 * image0) + weigh0, (32, 128))
    part = task_half_sum(image_part(image0, target), curve, core)
    alpha0 = norm0 / part[8][:, :1]
    residual_half = halves(target_blocks, core)[0] - alpha0[None] * part[:8]
    residual_blocks = whole(residual_half, core)
    residual = flat(residual_blocks)

    scalars = [total(residual * residual), total(diag * residual * residual), total(diag * residual * target)]
    rows = sum_over(with_scalars(product(residual, xs, 1), scalars), zhi_move)
    norm1, weigh1, cross = (rows[:, tokens + i : tokens + i + 1] for i in range(3))
    beta = norm1 / (norm0 + EPS)
    image1 = rows[:, :tokens] + beta * image0
    direction = residual + beta * target
    curve = gram_scale * total(image1 * image1) + weigh1 + 2.0 * beta * cross + beta * beta * weigh0

    def side_by_side(blocks):
        return blocks.transpose(2, 0, 1).reshape(-1, 128)

    def per_lane(column):
        return jnp.tile(column[:, 0], 4)[None]

    part = gram_scale * product(image1, xs, 0) + diag * direction
    part = side_by_side(part.reshape(32, 4, width).transpose(1, 0, 2)).reshape(16, 32, 128)
    curve = jnp.broadcast_to(per_lane(curve)[None], (16, 8, 128))
    total_part = jnp.sum(lax.all_to_all(jnp.concatenate([part, curve], axis=1), "task", 0, 0), axis=0)

    def mine_of(blocks):
        four = pick(blocks.reshape(4, 4, 32, 128), task // 4, 1)
        return side_by_side(lax.dynamic_slice_in_dim(four, 32 * (task % 4), 32, 2))

    my_target, my_residual = mine_of(target_blocks), mine_of(residual_blocks)
    alpha1 = per_lane(norm1) / total_part[32:33]
    merged = per_lane(alpha0) * my_target + alpha1 * (my_residual + per_lane(beta) * my_target)
    both = jnp.concatenate([merged, my_residual - alpha1 * total_part[:32]])

    two, three, one = staged(lambda k: both[:, 128 - 32 * k : 160 - 32 * k], x_move)
    groups = jnp.stack([both[:, :32], three, two, one])
    groups = lax.dynamic_slice_in_dim(jnp.concatenate([groups, groups]), (4 - x) % 4, 4, 0)
    result = groups.transpose(1, 0, 2).reshape(64, 128)
    return result[:32], result[32:]


def solution(mesh):
    in_specs = (P("task", None, "rows"), P("task", "rows", None))
    out_specs = (P(("rows", "task"), None), P(("rows", "task"), None))

    return jax.shard_map(on_device, mesh=mesh, in_specs=in_specs, out_specs=out_specs, check_vma=False)
```

```python
import jax
import jax.numpy as jnp
from jax import lax
from jax.sharding import PartitionSpec as P


ALPHA = 0.9
EPS = 1e-06


def moved(value, axis, to):
    return lax.ppermute(value, axis, [(i, to(i)) for i in range(16)])


def staged(value_of, move):
    arrived = []
    for k in (2, 3, 1):
        arrived.append(move(value_of(k), k))
    return arrived


def x_move(value, k):
    return moved(value, "rows", lambda r: r - r % 4 + (r + k) % 4)


def zhi_move(value, k):
    return moved(value, "rows", lambda r: (r + 4 * k) % 16)


def core_move(value):
    return moved(value, "task", lambda t: t ^ 1)


def zlo_move(value):
    return moved(value, "task", lambda t: t ^ 8)


def y_move(value, k):
    return moved(value, "task", lambda t: (t & 9) | ((((t >> 1) & 3) + k) % 4) << 1)


def sum_over(value, move):
    two, three, one = staged(lambda k: value, move)
    return value + one + three + two


def pick(value, index, dim=0):
    return lax.dynamic_index_in_dim(value, index, dim, keepdims=False)


def pieces(value):
    high = lax.reduce_precision(value, 8, 7)
    low = value - high
    return jnp.concatenate([high.astype(jnp.bfloat16), low.astype(jnp.bfloat16)], axis=0)


def product(value, x, dim):
    n = value.shape[0]
    wide = lax.dot_general(pieces(value), x, (((1,), (dim,)), ((), ())), preferred_element_type=jnp.float32)
    return wide[:n] + wide[n:]


def blocks_of(value):
    return value.reshape(value.shape[0], -1, 128).transpose(1, 0, 2)


def flat(blocks):
    return blocks.transpose(1, 0, 2).reshape(blocks.shape[1], -1)


def zlo_y_sum(blocks):
    return sum_over(blocks + zlo_move(blocks), y_move)


def with_scalars(value, scalars):
    lane = lax.broadcasted_iota(jnp.int32, (value.shape[0], 128), 1)
    extra = jnp.zeros((value.shape[0], 128), jnp.float32)
    for i, s in enumerate(scalars):
        extra = jnp.where(lane == i, s, extra)
    return jnp.concatenate([value, extra], axis=1)


def total(value):
    return jnp.sum(value, axis=1, keepdims=True)


def on_device(probes, task_weights):
    own_x = probes[0]
    w = task_weights[0]
    tokens, width = own_x.shape
    tasks = lax.axis_size("task")
    row = lax.axis_index("rows")
    task = lax.axis_index("task")
    x, core = row % 4, task % 2
    scale = 1.0 / (tokens * tasks)
    gram_scale, diag_scale = ALPHA * scale, (1.0 - ALPHA) * scale

    first = lax.dot_general(w, own_x, (((0,), (1,)), ((), ())), preferred_element_type=jnp.float32)
    first = first.reshape(4, 32, tokens)
    two, three, one = staged(lambda k: pick(first, (x + k) % 4), x_move)
    mine = pick(first, x) + one + three + two
    turned = w.T.reshape(4, 32, width)
    ws_far = x_move(pick(turned, (x + 2) % 4), 2)

    half = tokens // 2
    from_left = x_move(own_x, 1)
    from_right = x_move(own_x, 3)
    outputs = sum_over(mine, zhi_move)
    far_left = x_move(jnp.concatenate([from_left[:half], pick(turned, (x + 1) % 4)]), 1)
    far_right = x_move(jnp.concatenate([from_right[half:], pick(turned, (x + 3) % 4)]), 3)

    far = jnp.concatenate([far_left[:half], far_right[:half]])
    xs = lax.optimization_barrier(jnp.concatenate([own_x, from_left, far, from_right], axis=1))
    ws = jnp.concatenate([pick(turned, x), far_left[half:], ws_far, far_right[half:]], axis=1)
    wide_x = xs.astype(jnp.float32)
    diag = diag_scale * jnp.sum(wide_x * wide_x, axis=0, keepdims=True)

    part = blocks_of(gram_scale * product(outputs, xs, 0) + diag * ws.astype(jnp.float32))
    part = part.reshape(16, 2, 16, 128)
    other = core_move(pick(part, 1 - core, 1))
    target_blocks = zlo_y_sum(pick(part, core, 1) + other)
    target = flat(target_blocks)

    xs_other = core_move(xs)
    xs_other, diag = lax.optimization_barrier((xs_other, diag))
    wide_x = xs_other.astype(jnp.float32)
    diag = diag + diag_scale * jnp.sum(wide_x * wide_x, axis=0, keepdims=True)

    def outputs_of(vector):
        return jnp.concatenate([product(vector, xs, 1), product(vector, xs_other, 1)], axis=1)

    def image_of(y, vector):
        both = product(y[:, :tokens], xs, 0) + product(y[:, tokens:], xs_other, 0)
        return gram_scale * both + diag * vector

    def columns_of(rows, n):
        return rows[:, : 2 * tokens], *(rows[:, 2 * tokens + i : 2 * tokens + i + 1] for i in range(n))

    scalars = [total(target * target), total(diag * target * target)]
    rows = sum_over(with_scalars(outputs_of(target), scalars), zhi_move)
    image0, norm0, weigh0 = columns_of(rows, 2)
    curve = jnp.broadcast_to(gram_scale * total(image0 * image0) + weigh0, (1, 16, 128))
    part = blocks_of(image_of(image0, target))
    part = zlo_y_sum(jnp.concatenate([part, curve]))
    alpha0 = norm0 / part[16][:, :1]
    residual_blocks = target_blocks - alpha0[None] * part[:16]
    residual = flat(residual_blocks)

    scalars = [total(residual * residual), total(diag * residual * residual), total(diag * residual * target)]
    rows = sum_over(with_scalars(outputs_of(residual), scalars), zhi_move)
    image1, norm1, weigh1, cross = columns_of(rows, 3)
    beta = norm1 / (norm0 + EPS)
    image1 = image1 + beta * image0
    direction = residual + beta * target
    curve = gram_scale * total(image1 * image1) + weigh1 + 2.0 * beta * cross + beta * beta * weigh0

    part = image_of(image1, direction)
    part = part.reshape(16, 4, width).transpose(1, 0, 2).reshape(64, width).T.reshape(16, 2, 16, 64)
    part = part.transpose(0, 2, 1, 3).reshape(16, 16, 128)
    curve = jnp.broadcast_to(jnp.tile(curve[:, 0], 8)[None, None], (16, 8, 128))
    part = lax.all_to_all(jnp.concatenate([part, curve], axis=1), "task", 0, 0)
    part = jnp.sum(part.reshape(8, 2, 24, 128), axis=0)
    curve = part[:, 16, :16].reshape(32)
    part = part[:, :16].reshape(2, 16, 2, 4, 16).transpose(2, 1, 3, 0, 4).reshape(32, 128)

    def rows_of(device):
        def four(blocks):
            four = pick(blocks.reshape(4, 4, 16, 128), device // 4, 1)
            return lax.dynamic_slice_in_dim(four, 32 * (device % 4), 32, 2).reshape(64, 32)

        wide = [jnp.broadcast_to(column, (16, 32)) for column in (alpha0, beta, norm1)]
        return jnp.concatenate([four(target_blocks), four(residual_blocks)] + wide)

    other = core_move(rows_of(task ^ 1))
    own = rows_of(task)
    both = jnp.where(core == 0, jnp.stack([own, other]), jnp.stack([other, own]))

    def side_by_side(value):
        return value.reshape(2, 4, 16, 32).transpose(3, 1, 0, 2).reshape(32, 128)

    def per_lane(vector):
        return jnp.tile(vector, 4)[None]

    my_target, my_residual = side_by_side(both[:, :64]), side_by_side(both[:, 64:128])
    alpha0, beta, norm1 = (both[:, 128 + 16 * i : 144 + 16 * i, 0].reshape(32) for i in range(3))
    alpha1 = per_lane(norm1 / curve)
    merged = per_lane(alpha0) * my_target + alpha1 * (my_residual + per_lane(beta) * my_target)
    both = jnp.concatenate([merged, my_residual - alpha1 * part])

    two, three, one = staged(lambda k: both[:, 128 - 32 * k : 160 - 32 * k], x_move)
    groups = jnp.stack([both[:, :32], three, two, one])
    groups = lax.dynamic_slice_in_dim(jnp.concatenate([groups, groups]), (4 - x) % 4, 4, 0)
    result = groups.transpose(1, 0, 2).reshape(64, 128)
    return result[:32], result[32:]


def solution(mesh):
    in_specs = (P("task", None, "rows"), P("task", "rows", None))
    out_specs = (P(("rows", "task"), None), P(("rows", "task"), None))

    return jax.shard_map(on_device, mesh=mesh, in_specs=in_specs, out_specs=out_specs, check_vma=False)
```

```python
import jax
import jax.numpy as jnp
from jax import lax
from jax.sharding import PartitionSpec as P


ALPHA = 0.9
EPS = 1e-06


def moved(value, axis, to):
    return lax.ppermute(value, axis, [(i, to(i)) for i in range(16)])


def staged(value_of, move):
    arrived = []
    for k in (2, 3, 1):
        arrived.append(move(value_of(k), k))
    return arrived


def x_move(value, k):
    return moved(value, "rows", lambda r: r - r % 4 + (r + k) % 4)


def zhi_move(value, k):
    return moved(value, "rows", lambda r: (r + 4 * k) % 16)


def core_move(value):
    return moved(value, "task", lambda t: t ^ 1)


def zlo_move(value):
    return moved(value, "task", lambda t: t ^ 8)


def y_move(value, k):
    return moved(value, "task", lambda t: (t & 9) | ((((t >> 1) & 3) + k) % 4) << 1)


def sum_over(value, move):
    two, three, one = staged(lambda k: value, move)
    return value + one + three + two


def pick(value, index, dim=0):
    return lax.dynamic_index_in_dim(value, index, dim, keepdims=False)


def pieces(value):
    high = lax.reduce_precision(value, 8, 7)
    low = value - high
    return jnp.concatenate([high.astype(jnp.bfloat16), low.astype(jnp.bfloat16)], axis=0)


def product(value, x, dim):
    n = value.shape[0]
    wide = lax.dot_general(pieces(value), x, (((1,), (dim,)), ((), ())), preferred_element_type=jnp.float32)
    return wide[:n] + wide[n:]


def blocks_of(value):
    return value.reshape(value.shape[0], -1, 128).transpose(1, 0, 2)


def flat(blocks):
    return blocks.transpose(1, 0, 2).reshape(blocks.shape[1], -1)


def zlo_y_sum(blocks):
    return sum_over(blocks + zlo_move(blocks), y_move)


def with_scalars(value, scalars):
    lane = lax.broadcasted_iota(jnp.int32, (value.shape[0], 128), 1)
    extra = jnp.zeros((value.shape[0], 128), jnp.float32)
    for i, s in enumerate(scalars):
        extra = jnp.where(lane == i, s, extra)
    return jnp.concatenate([value, extra], axis=1)


def total(value):
    return jnp.sum(value, axis=1, keepdims=True)


def on_device(probes, task_weights):
    own_x = probes[0]
    w = task_weights[0]
    tokens, width = own_x.shape
    tasks = lax.axis_size("task")
    row = lax.axis_index("rows")
    task = lax.axis_index("task")
    x, core = row % 4, task % 2
    scale = 1.0 / (tokens * tasks)
    gram_scale, diag_scale = ALPHA * scale, (1.0 - ALPHA) * scale

    first = lax.dot_general(w, own_x, (((0,), (1,)), ((), ())), preferred_element_type=jnp.float32)
    first = first.reshape(4, 32, tokens)
    two, three, one = staged(lambda k: pick(first, (x + k) % 4), x_move)
    mine = pick(first, x) + one + three + two
    turned = w.T.reshape(4, 32, width)

    half = tokens // 2
    from_left = x_move(jnp.concatenate([own_x, pick(turned, (x + 2) % 4)]), 1)
    from_right = x_move(own_x, 3)
    outputs = sum_over(mine, zhi_move)
    far_left = jnp.concatenate([from_left[:half], from_left[tokens:], pick(turned, (x + 1) % 4)])
    far_left = x_move(far_left, 1)
    far_right = x_move(jnp.concatenate([from_right[half:], pick(turned, (x + 3) % 4)]), 3)

    def squares(value):
        wide = value.astype(jnp.float32)
        return diag_scale * jnp.sum(wide * wide, axis=0, keepdims=True)

    far = jnp.concatenate([far_left[:half], far_right[:half]])
    xs = lax.optimization_barrier(jnp.concatenate([own_x, from_left[:tokens], far, from_right], axis=1))
    ws = [pick(turned, x), far_left[half + 32 :], far_left[half : half + 32], far_right[half:]]
    ws = jnp.concatenate(ws, axis=1)
    diag = squares(xs)

    part = blocks_of(gram_scale * product(outputs, xs, 0) + diag * ws.astype(jnp.float32))
    part = part.reshape(16, 2, 16, 128)
    other = core_move(pick(part, 1 - core, 1))
    target_blocks = zlo_y_sum(pick(part, core, 1) + other)
    target = flat(target_blocks)

    xs_other = core_move(xs)
    xs_other, diag = lax.optimization_barrier((xs_other, diag))
    diag = diag + squares(xs_other)

    def outputs_of(vector):
        return jnp.concatenate([product(vector, xs, 1), product(vector, xs_other, 1)], axis=1)

    def image_of(y, vector):
        both = product(y[:, :tokens], xs, 0) + product(y[:, tokens:], xs_other, 0)
        return gram_scale * both + diag * vector

    def columns_of(rows, n):
        return rows[:, : 2 * tokens], *(rows[:, 2 * tokens + i : 2 * tokens + i + 1] for i in range(n))

    scalars = [total(target * target), total(diag * target * target)]
    rows = sum_over(with_scalars(outputs_of(target), scalars), zhi_move)
    image0, norm0, weigh0 = columns_of(rows, 2)
    curve = jnp.broadcast_to(gram_scale * total(image0 * image0) + weigh0, (1, 16, 128))
    part = blocks_of(image_of(image0, target))
    part = zlo_y_sum(jnp.concatenate([part, curve]))
    alpha0 = norm0 / part[16][:, :1]
    residual_blocks = target_blocks - alpha0[None] * part[:16]
    residual = flat(residual_blocks)

    scalars = [total(residual * residual), total(diag * residual * residual), total(diag * residual * target)]
    rows = sum_over(with_scalars(outputs_of(residual), scalars), zhi_move)
    image1, norm1, weigh1, cross = columns_of(rows, 3)
    beta = norm1 / (norm0 + EPS)
    image1 = image1 + beta * image0
    direction = residual + beta * target
    curve = gram_scale * total(image1 * image1) + weigh1 + 2.0 * beta * cross + beta * beta * weigh0

    part = image_of(image1, direction)
    part = part.reshape(16, 4, width).transpose(1, 0, 2).reshape(64, width).T.reshape(16, 2, 16, 64)
    part = part.transpose(0, 2, 1, 3).reshape(16, 16, 128)
    curve = jnp.broadcast_to(jnp.tile(curve[:, 0], 8)[None, None], (16, 8, 128))
    part = lax.all_to_all(jnp.concatenate([part, curve], axis=1), "task", 0, 0)
    part = jnp.sum(part.reshape(8, 2, 24, 128), axis=0)
    curve = part[:, 16, :16].reshape(32)
    part = part[:, :16].reshape(2, 16, 2, 4, 16).transpose(2, 1, 3, 0, 4).reshape(32, 128)

    def piece_of(blocks):
        return pick(blocks.reshape(4, 4, 16, 128), task // 4, 1)

    lane = lax.broadcasted_iota(jnp.int32, (16, 128), 1)
    scalars = jnp.where(lane < 32, alpha0, jnp.where(lane < 64, beta, norm1))
    own = jnp.concatenate([piece_of(target_blocks), piece_of(residual_blocks), scalars[None]])
    other = core_move(own)
    both = jnp.where(core == 0, jnp.stack([own, other]), jnp.stack([other, own]))
    alpha0, beta, norm1 = (both[:, 8, :, 32 * i].reshape(32) for i in range(3))
    both = lax.dynamic_slice_in_dim(both, 32 * (task % 4), 32, 3)

    def side_by_side(value):
        return value.transpose(3, 1, 0, 2).reshape(32, 128)

    def per_lane(vector):
        return jnp.tile(vector, 4)[None]

    my_target, my_residual = side_by_side(both[:, :4]), side_by_side(both[:, 4:8])
    alpha1 = per_lane(norm1 / curve)
    merged = per_lane(alpha0) * my_target + alpha1 * (my_residual + per_lane(beta) * my_target)
    both = jnp.concatenate([merged, my_residual - alpha1 * part])

    two, three, one = staged(lambda k: both[:, 128 - 32 * k : 160 - 32 * k], x_move)
    groups = jnp.stack([both[:, :32], three, two, one])
    groups = lax.dynamic_slice_in_dim(jnp.concatenate([groups, groups]), (4 - x) % 4, 4, 0)
    result = groups.transpose(1, 0, 2).reshape(64, 128)
    return result[:32], result[32:]


def solution(mesh):
    in_specs = (P("task", None, "rows"), P("task", "rows", None))
    out_specs = (P(("rows", "task"), None), P(("rows", "task"), None))

    return jax.shard_map(on_device, mesh=mesh, in_specs=in_specs, out_specs=out_specs, check_vma=False)
```

```python
import jax
import jax.numpy as jnp
from jax import lax
from jax.experimental.layout import Layout, with_layout_constraint
from jax.sharding import PartitionSpec as P


ALPHA = 0.9
EPS = 1e-06


def moved(value, axis, to):
    return lax.ppermute(value, axis, [(i, to(i)) for i in range(16)])


def staged(value_of, move):
    arrived = []
    for k in (2, 3, 1):
        arrived.append(move(value_of(k), k))
    return arrived


def x_move(value, k):
    return moved(value, "rows", lambda r: r - r % 4 + (r + k) % 4)


def zhi_move(value, k):
    return moved(value, "rows", lambda r: (r + 4 * k) % 16)


def core_move(value):
    return moved(value, "task", lambda t: t ^ 1)


def zlo_move(value):
    return moved(value, "task", lambda t: t ^ 8)


def y_move(value, k):
    return moved(value, "task", lambda t: (t & 9) | ((((t >> 1) & 3) + k) % 4) << 1)


def sum_over(value, move):
    two, three, one = staged(lambda k: value, move)
    return value + one + three + two


def pick(value, index, dim=0):
    return lax.dynamic_index_in_dim(value, index, dim, keepdims=False)


def pieces(value):
    high = lax.reduce_precision(value, 8, 7)
    low = value - high
    return jnp.concatenate([high.astype(jnp.bfloat16), low.astype(jnp.bfloat16)], axis=0)


def product(value, x, dim):
    n = value.shape[0]
    wide = lax.dot_general(pieces(value), x, (((1,), (dim,)), ((), ())), preferred_element_type=jnp.float32)
    return wide[:n] + wide[n:]


def blocks_of(value):
    return value.reshape(value.shape[0], -1, 128).transpose(1, 0, 2)


def flat(blocks):
    return blocks.transpose(1, 0, 2).reshape(blocks.shape[1], -1)


def zlo_y_sum(blocks):
    return sum_over(blocks + zlo_move(blocks), y_move)


def with_scalars(value, scalars):
    lane = lax.broadcasted_iota(jnp.int32, (value.shape[0], 128), 1)
    extra = jnp.zeros((value.shape[0], 128), jnp.float32)
    for i, s in enumerate(scalars):
        extra = jnp.where(lane == i, s, extra)
    return jnp.concatenate([value, extra], axis=1)


def total(value):
    return jnp.sum(value, axis=1, keepdims=True)


def on_device(probes, task_weights):
    own_x = probes[0]
    w = task_weights[0]
    tokens, width = own_x.shape
    tasks = lax.axis_size("task")
    row = lax.axis_index("rows")
    task = lax.axis_index("task")
    x, core = row % 4, task % 2
    scale = 1.0 / (tokens * tasks)
    gram_scale, diag_scale = ALPHA * scale, (1.0 - ALPHA) * scale

    first = lax.dot_general(w, own_x, (((0,), (1,)), ((), ())), preferred_element_type=jnp.float32)
    first = first.reshape(4, 32, tokens)
    two, three, one = staged(lambda k: pick(first, (x + k) % 4), x_move)
    mine = pick(first, x) + one + three + two
    turned = w.T.reshape(4, 32, width)

    half = tokens // 2
    from_left = x_move(jnp.concatenate([own_x, pick(turned, (x + 2) % 4)]), 1)
    from_right = x_move(own_x, 3)
    outputs = sum_over(mine, zhi_move)
    far_left = jnp.concatenate([from_left[:half], from_left[tokens:], pick(turned, (x + 1) % 4)])
    far_left = x_move(far_left, 1)
    far_right = x_move(jnp.concatenate([from_right[half:], pick(turned, (x + 3) % 4)]), 3)

    def squares(value):
        wide = value.astype(jnp.float32)
        return diag_scale * jnp.sum(wide * wide, axis=0, keepdims=True)

    far = jnp.concatenate([far_left[:half], far_right[:half]])
    xs = lax.optimization_barrier(jnp.concatenate([own_x, from_left[:tokens], far, from_right], axis=1))
    ws = [pick(turned, x), far_left[half + 32 :], far_left[half : half + 32], far_right[half:]]
    ws = jnp.concatenate(ws, axis=1)
    diag = squares(xs)

    part = blocks_of(gram_scale * product(outputs, xs, 0) + diag * ws.astype(jnp.float32))
    part = part.reshape(16, 2, 16, 128)
    other = core_move(pick(part, 1 - core, 1))
    target_blocks = zlo_y_sum(pick(part, core, 1) + other)
    target = flat(target_blocks)

    xs_other = core_move(xs)
    xs_other, diag = lax.optimization_barrier((xs_other, diag))
    diag = diag + squares(xs_other)

    def outputs_of(vector):
        return jnp.concatenate([product(vector, xs, 1), product(vector, xs_other, 1)], axis=1)

    def image_of(y, vector):
        both = product(y[:, :tokens], xs, 0) + product(y[:, tokens:], xs_other, 0)
        return gram_scale * both + diag * vector

    def columns_of(rows, n):
        return rows[:, : 2 * tokens], *(rows[:, 2 * tokens + i : 2 * tokens + i + 1] for i in range(n))

    scalars = [total(target * target), total(diag * target * target)]
    rows = sum_over(with_scalars(outputs_of(target), scalars), zhi_move)
    image0, norm0, weigh0 = columns_of(rows, 2)
    curve = jnp.broadcast_to(gram_scale * total(image0 * image0) + weigh0, (1, 16, 128))
    part = blocks_of(image_of(image0, target))
    part = zlo_y_sum(jnp.concatenate([part, curve]))
    alpha0 = norm0 / part[16][:, :1]
    residual_blocks = target_blocks - alpha0[None] * part[:16]
    residual = flat(residual_blocks)

    scalars = [total(residual * residual), total(diag * residual * residual), total(diag * residual * target)]
    rows = sum_over(with_scalars(outputs_of(residual), scalars), zhi_move)
    image1, norm1, weigh1, cross = columns_of(rows, 3)
    beta = norm1 / (norm0 + EPS)
    image1 = image1 + beta * image0
    direction = residual + beta * target
    curve = gram_scale * total(image1 * image1) + weigh1 + 2.0 * beta * cross + beta * beta * weigh0

    part = image_of(image1, direction)
    part = part.reshape(16, 4, width).transpose(1, 0, 2).reshape(64, width).T.reshape(16, 2, 16, 64)
    part = part.transpose(0, 2, 1, 3).reshape(16, 16, 128)
    curve = jnp.broadcast_to(jnp.tile(curve[:, 0], 8)[None, None], (16, 8, 128))
    part = lax.all_to_all(jnp.concatenate([part, curve], axis=1), "task", 0, 0)
    part = jnp.sum(part.reshape(8, 2, 24, 128), axis=0)
    curve = part[:, 16, :16].reshape(32)
    part = part[:, :16].reshape(2, 16, 2, 4, 16).transpose(2, 1, 3, 0, 4).reshape(32, 128)

    def piece_of(blocks):
        return pick(blocks.reshape(4, 4, 16, 128), task // 4, 1)

    lane = lax.broadcasted_iota(jnp.int32, (16, 128), 1)
    scalars = jnp.where(lane < 32, alpha0, jnp.where(lane < 64, beta, norm1))
    own = jnp.concatenate([piece_of(target_blocks), piece_of(residual_blocks), scalars[None]])
    other = core_move(own)
    both = jnp.where(core == 0, jnp.stack([own, other]), jnp.stack([other, own]))
    alpha0, beta, norm1 = (both[:, 8, :, 32 * i].reshape(32) for i in range(3))
    both = lax.dynamic_slice_in_dim(both, 32 * (task % 4), 32, 3)

    def side_by_side(value):
        return value.transpose(3, 1, 0, 2).reshape(32, 128)

    def per_lane(vector):
        return jnp.tile(vector, 4)[None]

    my_target, my_residual = side_by_side(both[:, :4]), side_by_side(both[:, 4:8])
    alpha1 = per_lane(norm1 / curve)
    merged = per_lane(alpha0) * my_target + alpha1 * (my_residual + per_lane(beta) * my_target)
    both = jnp.concatenate([merged, my_residual - alpha1 * part])

    mine = lax.broadcasted_iota(jnp.int32, (64, 128), 1) // 32 == x

    turns = jnp.stack([jnp.roll(both, 32 * k, axis=1) for k in range(4)])

    def placed(k):
        piece = jnp.where(mine, pick(turns, (x - k) % 4), 0.0)
        return with_layout_constraint(piece, Layout(major_to_minor=(0, 1)))

    two, three, one = staged(lambda k: placed(4 - k), x_move)
    result = placed(0) + three + two + one
    return result[:32], result[32:]


def solution(mesh):
    in_specs = (P("task", None, "rows"), P("task", "rows", None))
    out_specs = (P(("rows", "task"), None), P(("rows", "task"), None))

    return jax.shard_map(on_device, mesh=mesh, in_specs=in_specs, out_specs=out_specs, check_vma=False)
```

```python
import jax
import jax.numpy as jnp
from jax import lax
from jax.sharding import PartitionSpec as P


ALPHA = 0.9
EPS = 1e-06


def moved(value, axis, to):
    return lax.ppermute(value, axis, [(i, to(i)) for i in range(16)])


def staged(value_of, move):
    arrived = []
    for k in (2, 3, 1):
        arrived.append(move(value_of(k), k))
    return arrived


def x_move(value, k):
    return moved(value, "rows", lambda r: r - r % 4 + (r + k) % 4)


def zhi_move(value, k):
    return moved(value, "rows", lambda r: (r + 4 * k) % 16)


def core_move(value):
    return moved(value, "task", lambda t: t ^ 1)


def zlo_move(value):
    return moved(value, "task", lambda t: t ^ 8)


def y_move(value, k):
    return moved(value, "task", lambda t: (t & 9) | ((((t >> 1) & 3) + k) % 4) << 1)


def sum_over(value, move):
    two, three, one = staged(lambda k: value, move)
    return value + one + three + two


def pick(value, index, dim=0):
    return lax.dynamic_index_in_dim(value, index, dim, keepdims=False)


def pieces(value):
    high = lax.reduce_precision(value, 8, 7)
    low = value - high
    return jnp.concatenate([high.astype(jnp.bfloat16), low.astype(jnp.bfloat16)], axis=0)


def product(value, x, dim):
    n = value.shape[0]
    wide = lax.dot_general(pieces(value), x, (((1,), (dim,)), ((), ())), preferred_element_type=jnp.float32)
    return wide[:n] + wide[n:]


def blocks_of(value):
    return value.reshape(value.shape[0], -1, 128).transpose(1, 0, 2)


def flat(blocks):
    return blocks.transpose(1, 0, 2).reshape(blocks.shape[1], -1)


def zlo_y_sum(blocks):
    return sum_over(blocks + zlo_move(blocks), y_move)


def with_scalars(value, scalars):
    lane = lax.broadcasted_iota(jnp.int32, (value.shape[0], 128), 1)
    extra = jnp.zeros((value.shape[0], 128), jnp.float32)
    for i, s in enumerate(scalars):
        extra = jnp.where(lane == i, s, extra)
    return jnp.concatenate([value, extra], axis=1)


def total(value):
    return jnp.sum(value, axis=1, keepdims=True)


def on_device(probes, task_weights):
    own_x = probes[0]
    w = task_weights[0]
    tokens, width = own_x.shape
    tasks = lax.axis_size("task")
    row = lax.axis_index("rows")
    task = lax.axis_index("task")
    x, core = row % 4, task % 2
    scale = 1.0 / (tokens * tasks)
    gram_scale, diag_scale = ALPHA * scale, (1.0 - ALPHA) * scale

    first = lax.optimization_barrier(jnp.dot(own_x, w, preferred_element_type=jnp.float32))
    first = first.T.reshape(4, 32, tokens)
    two, three, one = staged(lambda k: pick(first, (x + k) % 4), x_move)
    mine = pick(first, x) + one + three + two
    turned = w.T.reshape(4, 32, width)

    half = tokens // 2
    from_left = x_move(jnp.concatenate([own_x, pick(turned, (x + 2) % 4)]), 1)
    from_right = x_move(own_x, 3)
    outputs = sum_over(mine, zhi_move)
    far_left = jnp.concatenate([from_left[:half], from_left[tokens:], pick(turned, (x + 1) % 4)])
    far_left = x_move(far_left, 1)
    far_right = x_move(jnp.concatenate([from_right[half:], pick(turned, (x + 3) % 4)]), 3)

    def squares(value):
        wide = value.astype(jnp.float32)
        return diag_scale * jnp.sum(wide * wide, axis=0, keepdims=True)

    far = jnp.concatenate([far_left[:half], far_right[:half]])
    blocks = [own_x, from_left[:tokens], far, from_right]
    ws = [pick(turned, x), far_left[half + 32 :], far_left[half : half + 32], far_right[half:]]
    diags = [squares(block) for block in blocks]
    part = [
        gram_scale * product(outputs, block, 0) + d * piece.astype(jnp.float32)
        for block, d, piece in zip(blocks, diags, ws)
    ]
    part = jnp.concatenate([blocks_of(block) for block in part])
    xs = lax.optimization_barrier(jnp.concatenate(blocks, axis=1))
    diag = jnp.concatenate(diags, axis=1)

    part = part.reshape(16, 2, 16, 128)
    other = core_move(pick(part, 1 - core, 1))
    target_blocks = zlo_y_sum(pick(part, core, 1) + other)
    target = flat(target_blocks)

    xs_other = core_move(xs)
    xs_other, diag = lax.optimization_barrier((xs_other, diag))
    diag = diag + squares(xs_other)

    def outputs_of(vector):
        return jnp.concatenate([product(vector, xs, 1), product(vector, xs_other, 1)], axis=1)

    def image_of(y, vector):
        both = product(y[:, :tokens], xs, 0) + product(y[:, tokens:], xs_other, 0)
        return gram_scale * both + diag * vector

    def columns_of(rows, n):
        return rows[:, : 2 * tokens], *(rows[:, 2 * tokens + i : 2 * tokens + i + 1] for i in range(n))

    scalars = [total(target * target), total(diag * target * target)]
    rows = sum_over(with_scalars(outputs_of(target), scalars), zhi_move)
    image0, norm0, weigh0 = columns_of(rows, 2)
    curve = jnp.broadcast_to(gram_scale * total(image0 * image0) + weigh0, (1, 16, 128))
    part = blocks_of(image_of(image0, target))
    part = zlo_y_sum(jnp.concatenate([part, curve]))
    alpha0 = norm0 / part[16][:, :1]
    residual_blocks = target_blocks - alpha0[None] * part[:16]
    residual = flat(residual_blocks)

    scalars = [total(residual * residual), total(diag * residual * residual), total(diag * residual * target)]
    rows = sum_over(with_scalars(outputs_of(residual), scalars), zhi_move)
    image1, norm1, weigh1, cross = columns_of(rows, 3)
    beta = norm1 / (norm0 + EPS)
    image1 = image1 + beta * image0
    direction = residual + beta * target
    curve = gram_scale * total(image1 * image1) + weigh1 + 2.0 * beta * cross + beta * beta * weigh0

    part = image_of(image1, direction)
    part = part.reshape(16, 4, width).transpose(1, 0, 2).reshape(64, width).T.reshape(16, 2, 16, 64)
    part = part.transpose(0, 2, 1, 3).reshape(16, 16, 128)
    curve = jnp.broadcast_to(jnp.tile(curve[:, 0], 8)[None, None], (16, 8, 128))
    part = lax.all_to_all(jnp.concatenate([part, curve], axis=1), "task", 0, 0)
    part = jnp.sum(part.reshape(8, 2, 24, 128), axis=0)
    curve = part[:, 16, :16].reshape(32)
    part = part[:, :16].reshape(2, 16, 2, 4, 16).transpose(2, 1, 3, 0, 4).reshape(32, 128)

    def piece_of(blocks):
        return pick(blocks.reshape(4, 4, 16, 128), task // 4, 1)

    lane = lax.broadcasted_iota(jnp.int32, (16, 128), 1)
    scalars = jnp.where(lane < 32, alpha0, jnp.where(lane < 64, beta, norm1))
    own = jnp.concatenate([piece_of(target_blocks), piece_of(residual_blocks), scalars[None]])
    other = core_move(own)
    both = jnp.where(core == 0, jnp.stack([own, other]), jnp.stack([other, own]))
    alpha0, beta, norm1 = (both[:, 8, :, 32 * i].reshape(32) for i in range(3))
    both = lax.dynamic_slice_in_dim(both, 32 * (task % 4), 32, 3)

    def side_by_side(value):
        return value.transpose(3, 1, 0, 2).reshape(32, 128)

    def per_lane(vector):
        return jnp.tile(vector, 4)[None]

    my_target, my_residual = side_by_side(both[:, :4]), side_by_side(both[:, 4:8])
    alpha1 = per_lane(norm1 / curve)
    merged = per_lane(alpha0) * my_target + alpha1 * (my_residual + per_lane(beta) * my_target)
    both = jnp.concatenate([merged, my_residual - alpha1 * part])

    two, three, one = staged(lambda k: both[:, 128 - 32 * k : 160 - 32 * k], x_move)
    groups = jnp.stack([both[:, :32], three, two, one])
    groups = lax.dynamic_slice_in_dim(jnp.concatenate([groups, groups]), (4 - x) % 4, 4, 0)
    result = groups.transpose(1, 0, 2).reshape(64, 128)
    return result[:32], result[32:]


def solution(mesh):
    in_specs = (P("task", None, "rows"), P("task", "rows", None))
    out_specs = (P(("rows", "task"), None), P(("rows", "task"), None))

    return jax.shard_map(on_device, mesh=mesh, in_specs=in_specs, out_specs=out_specs, check_vma=False)
```

```python
import jax
import jax.numpy as jnp
from jax import lax
from jax.sharding import PartitionSpec as P


ALPHA = 0.9
EPS = 1e-06


def moved(value, axis, to):
    return lax.ppermute(value, axis, [(i, to(i)) for i in range(16)])


def staged(value_of, move):
    arrived = []
    for k in (2, 3, 1):
        arrived.append(move(value_of(k), k))
    return arrived


def x_move(value, k):
    return moved(value, "rows", lambda r: r - r % 4 + (r + k) % 4)


def zhi_move(value, k):
    return moved(value, "rows", lambda r: (r + 4 * k) % 16)


def core_move(value):
    return moved(value, "task", lambda t: t ^ 1)


def zlo_move(value):
    return moved(value, "task", lambda t: t ^ 8)


def y_move(value, k):
    return moved(value, "task", lambda t: (t & 9) | ((((t >> 1) & 3) + k) % 4) << 1)


def sum_over(value, move):
    two, three, one = staged(lambda k: value, move)
    return value + one + three + two


def pick(value, index, dim=0):
    return lax.dynamic_index_in_dim(value, index, dim, keepdims=False)


def pieces(value):
    high = lax.reduce_precision(value, 8, 7)
    low = value - high
    return jnp.concatenate([high.astype(jnp.bfloat16), low.astype(jnp.bfloat16)], axis=0)


def product(value, x, dim):
    n = value.shape[0]
    wide = lax.dot_general(pieces(value), x, (((1,), (dim,)), ((), ())), preferred_element_type=jnp.float32)
    return wide[:n] + wide[n:]


def blocks_of(value):
    return value.reshape(value.shape[0], -1, 128).transpose(1, 0, 2)


def flat(blocks):
    return blocks.transpose(1, 0, 2).reshape(blocks.shape[1], -1)


def zlo_y_sum(blocks):
    return sum_over(blocks + zlo_move(blocks), y_move)


def with_scalars(value, scalars):
    lane = lax.broadcasted_iota(jnp.int32, (value.shape[0], 128), 1)
    extra = jnp.zeros((value.shape[0], 128), jnp.float32)
    for i, s in enumerate(scalars):
        extra = jnp.where(lane == i, s, extra)
    return jnp.concatenate([value, extra], axis=1)


def total(value):
    return jnp.sum(value, axis=1, keepdims=True)


def on_device(probes, task_weights):
    own_x = probes[0]
    w = task_weights[0]
    tokens, width = own_x.shape
    tasks = lax.axis_size("task")
    row = lax.axis_index("rows")
    task = lax.axis_index("task")
    x, core = row % 4, task % 2
    scale = 1.0 / (tokens * tasks)
    gram_scale, diag_scale = ALPHA * scale, (1.0 - ALPHA) * scale

    first = lax.optimization_barrier(jnp.dot(own_x, w, preferred_element_type=jnp.float32))
    first = first.T.reshape(4, 32, tokens)
    two, three, one = staged(lambda k: pick(first, (x + k) % 4), x_move)
    mine = pick(first, x) + one + three + two
    turned = w.T.reshape(4, 32, width)

    half = tokens // 2
    from_left = x_move(jnp.concatenate([own_x, pick(turned, (x + 2) % 4)]), 1)
    from_right = x_move(own_x, 3)
    outputs = sum_over(mine, zhi_move)
    far_left = jnp.concatenate([from_left[:half], from_left[tokens:], pick(turned, (x + 1) % 4)])
    far_left = x_move(far_left, 1)
    far_right = x_move(jnp.concatenate([from_right[half:], pick(turned, (x + 3) % 4)]), 3)

    def squares(value):
        wide = value.astype(jnp.float32)
        return diag_scale * jnp.sum(wide * wide, axis=0, keepdims=True)

    far = jnp.concatenate([far_left[:half], far_right[:half]])
    blocks = [own_x, from_left[:tokens], far, from_right]
    ws = [pick(turned, x), far_left[half + 32 :], far_left[half : half + 32], far_right[half:]]
    diags = [squares(block) for block in blocks]
    part = [
        gram_scale * product(outputs, block, 0) + d * piece.astype(jnp.float32)
        for block, d, piece in zip(blocks, diags, ws)
    ]
    part = jnp.concatenate([blocks_of(block) for block in part])
    xs = lax.optimization_barrier(jnp.concatenate(blocks, axis=1))
    diag = jnp.concatenate(diags, axis=1)

    part = part.reshape(16, 2, 16, 128)
    other = core_move(pick(part, 1 - core, 1))
    target_blocks = zlo_y_sum(pick(part, core, 1) + other)
    target = flat(target_blocks)

    xs_other = core_move(xs)
    xs_other, diag = lax.optimization_barrier((xs_other, diag))
    diag = diag + squares(xs_other)

    def outputs_of(vector):
        return jnp.concatenate([product(vector, xs, 1), product(vector, xs_other, 1)], axis=1)

    def image_of(y, vector):
        both = product(y[:, :tokens], xs, 0) + product(y[:, tokens:], xs_other, 0)
        return gram_scale * both + diag * vector

    def columns_of(rows, n):
        return rows[:, : 2 * tokens], *(rows[:, 2 * tokens + i : 2 * tokens + i + 1] for i in range(n))

    scalars = [total(target * target), total(diag * target * target)]
    rows = sum_over(with_scalars(outputs_of(target), scalars), zhi_move)
    image0, norm0, weigh0 = columns_of(rows, 2)
    curve = jnp.broadcast_to(gram_scale * total(image0 * image0) + weigh0, (1, 16, 128))
    part = blocks_of(image_of(image0, target))
    part = zlo_y_sum(jnp.concatenate([part, curve]))
    alpha0 = norm0 / part[16][:, :1]
    residual_blocks = target_blocks - alpha0[None] * part[:16]
    residual = flat(residual_blocks)

    def piece_of(blocks):
        return pick(blocks.reshape(4, 4, 16, 128), task // 4, 1)

    own = jnp.concatenate([piece_of(target_blocks), piece_of(residual_blocks)])
    other = core_move(own)
    both = jnp.where(core == 0, jnp.stack([own, other]), jnp.stack([other, own]))
    both = lax.dynamic_slice_in_dim(both, 32 * (task % 4), 32, 3)
    my_target, my_residual = (both[:, i : i + 4].transpose(3, 1, 0, 2).reshape(32, 128) for i in (0, 4))

    scalars = [total(residual * residual), total(diag * residual * residual), total(diag * residual * target)]
    rows = sum_over(with_scalars(outputs_of(residual), scalars), zhi_move)
    rows, my_target, my_residual = lax.optimization_barrier((rows, my_target, my_residual))
    image1, norm1, weigh1, cross = columns_of(rows, 3)
    beta = norm1 / (norm0 + EPS)
    image1 = image1 + beta * image0
    direction = residual + beta * target
    curve = gram_scale * total(image1 * image1) + weigh1 + 2.0 * beta * cross + beta * beta * weigh0

    part = image_of(image1, direction)
    part = part.reshape(16, 4, width).transpose(1, 0, 2).reshape(64, width).T.reshape(16, 2, 16, 64)
    part = part.transpose(0, 2, 1, 3).reshape(16, 16, 128)
    scalars = [jnp.tile(column[:, 0], 8)[None] for column in (curve, alpha0, beta, norm1)]
    scalars = jnp.concatenate(scalars + [jnp.zeros((4, 128), jnp.float32)])
    scalars = jnp.broadcast_to(scalars[None], (16, 8, 128))
    part = lax.all_to_all(jnp.concatenate([part, scalars], axis=1), "task", 0, 0).reshape(8, 2, 24, 128)
    alpha0, beta, norm1 = (part[0, :, i, :16].reshape(32) for i in (17, 18, 19))
    part = jnp.sum(part, axis=0)
    curve = part[:, 16, :16].reshape(32)
    part = part[:, :16].reshape(2, 16, 2, 4, 16).transpose(2, 1, 3, 0, 4).reshape(32, 128)

    def per_lane(vector):
        return jnp.tile(vector, 4)[None]

    alpha1 = per_lane(norm1 / curve)
    merged = per_lane(alpha0) * my_target + alpha1 * (my_residual + per_lane(beta) * my_target)
    both = jnp.concatenate([merged, my_residual - alpha1 * part])

    two, three, one = staged(lambda k: both[:, 128 - 32 * k : 160 - 32 * k], x_move)
    groups = jnp.stack([both[:, :32], three, two, one])
    groups = lax.dynamic_slice_in_dim(jnp.concatenate([groups, groups]), (4 - x) % 4, 4, 0)
    result = groups.transpose(1, 0, 2).reshape(64, 128)
    return result[:32], result[32:]


def solution(mesh):
    in_specs = (P("task", None, "rows"), P("task", "rows", None))
    out_specs = (P(("rows", "task"), None), P(("rows", "task"), None))

    return jax.shard_map(on_device, mesh=mesh, in_specs=in_specs, out_specs=out_specs, check_vma=False)
```

```python
import jax
import jax.numpy as jnp
from jax import lax
from jax.experimental.layout import Layout, with_layout_constraint
from jax.sharding import PartitionSpec as P


ALPHA = 0.9
EPS = 1e-06


def moved(value, axis, to):
    return lax.ppermute(value, axis, [(i, to(i)) for i in range(16)])


def staged(value_of, move):
    arrived = []
    for k in (2, 3, 1):
        arrived.append(move(value_of(k), k))
    return arrived


def x_move(value, k):
    return moved(value, "rows", lambda r: r - r % 4 + (r + k) % 4)


def zhi_move(value, k):
    return moved(value, "rows", lambda r: (r + 4 * k) % 16)


def core_move(value):
    return moved(value, "task", lambda t: t ^ 1)


def zlo_move(value):
    return moved(value, "task", lambda t: t ^ 8)


def y_move(value, k):
    return moved(value, "task", lambda t: (t & 9) | ((((t >> 1) & 3) + k) % 4) << 1)


def sum_over(value, move):
    two, three, one = staged(lambda k: value, move)
    return value + one + three + two


def pick(value, index, dim=0):
    return lax.dynamic_index_in_dim(value, index, dim, keepdims=False)


def pieces(value):
    high = lax.reduce_precision(value, 8, 7)
    low = value - high
    return jnp.concatenate([high.astype(jnp.bfloat16), low.astype(jnp.bfloat16)], axis=0)


def product(value, x, dim):
    n = value.shape[0]
    wide = lax.dot_general(pieces(value), x, (((1,), (dim,)), ((), ())), preferred_element_type=jnp.float32)
    return wide[:n] + wide[n:]


def blocks_of(value):
    return value.reshape(value.shape[0], -1, 128).transpose(1, 0, 2)


def flat(blocks):
    return blocks.transpose(1, 0, 2).reshape(blocks.shape[1], -1)


def zlo_y_sum(blocks):
    return sum_over(blocks + zlo_move(blocks), y_move)


def with_scalars(value, scalars):
    lane = lax.broadcasted_iota(jnp.int32, (value.shape[0], 128), 1)
    extra = jnp.zeros((value.shape[0], 128), jnp.float32)
    for i, s in enumerate(scalars):
        extra = jnp.where(lane == i, s, extra)
    return jnp.concatenate([value, extra], axis=1)


def total(value):
    return jnp.sum(value, axis=1, keepdims=True)


def on_device(probes, task_weights):
    own_x = probes[0]
    w = task_weights[0]
    tokens, width = own_x.shape
    tasks = lax.axis_size("task")
    row = lax.axis_index("rows")
    task = lax.axis_index("task")
    x, core = row % 4, task % 2
    scale = 1.0 / (tokens * tasks)
    gram_scale, diag_scale = ALPHA * scale, (1.0 - ALPHA) * scale

    first = lax.optimization_barrier(jnp.dot(own_x, w, preferred_element_type=jnp.float32))
    first = first.T.reshape(4, 32, tokens)
    two, three, one = staged(lambda k: pick(first, (x + k) % 4), x_move)
    mine = pick(first, x) + one + three + two
    turned = w.T.reshape(4, 32, width)

    half = tokens // 2
    from_left = x_move(jnp.concatenate([own_x, pick(turned, (x + 2) % 4)]), 1)
    from_right = x_move(own_x, 3)
    outputs = sum_over(mine, zhi_move)
    far_left = jnp.concatenate([from_left[:half], from_left[tokens:], pick(turned, (x + 1) % 4)])
    far_left = x_move(far_left, 1)
    far_right = x_move(jnp.concatenate([from_right[half:], pick(turned, (x + 3) % 4)]), 3)

    def squares(value):
        wide = value.astype(jnp.float32)
        return diag_scale * jnp.sum(wide * wide, axis=0, keepdims=True)

    far = jnp.concatenate([far_left[:half], far_right[:half]])
    blocks = [own_x, from_left[:tokens], far, from_right]
    ws = [pick(turned, x), far_left[half + 32 :], far_left[half : half + 32], far_right[half:]]
    diags = [squares(block) for block in blocks]
    part = [
        gram_scale * product(outputs, block, 0) + d * piece.astype(jnp.float32)
        for block, d, piece in zip(blocks, diags, ws)
    ]
    part = jnp.concatenate([blocks_of(block) for block in part])
    xs = lax.optimization_barrier(jnp.concatenate(blocks, axis=1))
    diag = jnp.concatenate(diags, axis=1)

    part = part.reshape(16, 2, 16, 128)
    other = core_move(pick(part, 1 - core, 1))
    target_blocks = zlo_y_sum(pick(part, core, 1) + other)
    target = flat(target_blocks)

    xs_other = core_move(xs)
    xs_other, diag = lax.optimization_barrier((xs_other, diag))
    diag = diag + squares(xs_other)

    def outputs_of(vector):
        return jnp.concatenate([product(vector, xs, 1), product(vector, xs_other, 1)], axis=1)

    def image_of(y, vector):
        both = product(y[:, :tokens], xs, 0) + product(y[:, tokens:], xs_other, 0)
        return gram_scale * both + diag * vector

    def columns_of(rows, n):
        return rows[:, : 2 * tokens], *(rows[:, 2 * tokens + i : 2 * tokens + i + 1] for i in range(n))

    scalars = [total(target * target), total(diag * target * target)]
    rows = sum_over(with_scalars(outputs_of(target), scalars), zhi_move)
    image0, norm0, weigh0 = columns_of(rows, 2)
    curve = jnp.broadcast_to(gram_scale * total(image0 * image0) + weigh0, (1, 16, 128))
    part = blocks_of(image_of(image0, target))
    part = zlo_y_sum(jnp.concatenate([part, curve]))
    alpha0 = norm0 / part[16][:, :1]
    residual_blocks = target_blocks - alpha0[None] * part[:16]
    residual = flat(residual_blocks)

    scalars = [total(residual * residual), total(diag * residual * residual), total(diag * residual * target)]
    rows = sum_over(with_scalars(outputs_of(residual), scalars), zhi_move)
    image1, norm1, weigh1, cross = columns_of(rows, 3)
    beta = norm1 / (norm0 + EPS)
    image1 = image1 + beta * image0
    direction = residual + beta * target
    curve = gram_scale * total(image1 * image1) + weigh1 + 2.0 * beta * cross + beta * beta * weigh0

    part = image_of(image1, direction)
    part = part.reshape(16, 4, width).transpose(1, 0, 2).reshape(64, width).T.reshape(16, 2, 16, 64)
    part = part.transpose(0, 2, 1, 3).reshape(16, 16, 128)
    curve = jnp.broadcast_to(jnp.tile(curve[:, 0], 8)[None, None], (16, 8, 128))
    part = lax.all_to_all(jnp.concatenate([part, curve], axis=1), "task", 0, 0)
    part = jnp.sum(part.reshape(8, 2, 24, 128), axis=0)
    curve = part[:, 16, :16].reshape(32)
    part = part[:, :16].reshape(2, 16, 2, 4, 16).transpose(2, 1, 3, 0, 4).reshape(32, 128)

    def piece_of(blocks):
        return pick(blocks.reshape(4, 4, 16, 128), task // 4, 1)

    lane = lax.broadcasted_iota(jnp.int32, (16, 128), 1)
    scalars = jnp.where(lane < 32, alpha0, jnp.where(lane < 64, beta, norm1))
    own = jnp.concatenate([piece_of(target_blocks), piece_of(residual_blocks), scalars[None]])
    other = core_move(own)
    both = jnp.where(core == 0, jnp.stack([own, other]), jnp.stack([other, own]))
    alpha0, beta, norm1 = (both[:, 8, :, 32 * i].reshape(32) for i in range(3))
    both = lax.dynamic_slice_in_dim(both, 32 * (task % 4), 32, 3)

    def side_by_side(value):
        return value.transpose(3, 1, 0, 2).reshape(32, 128)

    def per_lane(vector):
        return jnp.tile(vector, 4)[None]

    my_target, my_residual = side_by_side(both[:, :4]), side_by_side(both[:, 4:8])
    alpha1 = per_lane(norm1 / curve)
    merged = per_lane(alpha0) * my_target + alpha1 * (my_residual + per_lane(beta) * my_target)
    both = jnp.concatenate([merged, my_residual - alpha1 * part])

    mine = lax.broadcasted_iota(jnp.int32, (64, 128), 1) // 32 == x

    turns = jnp.stack([jnp.roll(both, 32 * k, axis=1) for k in range(4)])

    def placed(k):
        piece = jnp.where(mine, pick(turns, (x - k) % 4), 0.0)
        return with_layout_constraint(piece, Layout(major_to_minor=(0, 1)))

    two, three, one = staged(lambda k: placed(4 - k), x_move)
    result = placed(0) + three + two + one
    return result[:32], result[32:]


def solution(mesh):
    in_specs = (P("task", None, "rows"), P("task", "rows", None))
    out_specs = (P(("rows", "task"), None), P(("rows", "task"), None))

    return jax.shard_map(on_device, mesh=mesh, in_specs=in_specs, out_specs=out_specs, check_vma=False)
```
